512 devices in a mesh: dp: 16 (over y_hi, x, core), seq: 32 (over z, y_lo).
Axes of the slice: x: 4, y: 8 (y_hi: 2, y_lo: 4; y = y_hi * 4 + y_lo), z: 8, core: 2. Of those that a mesh axis runs over, the one named last changes fastest.
Arguments:
- pre_gate: bfloat16 [16, 4096, 2048], P('dp', 'seq'), may hold values from -6 to 6
- post_gate: bfloat16 [16, 4096, 2048], P('dp', 'seq'), may hold values from -6 to 6
- values: bfloat16 [16, 4096, 2048], P('dp', 'seq'), may hold values from -6 to 6
- cotangent: bfloat16 [16, 4096, 2048], P('dp', 'seq'), may hold values from -6 to 6
- filters: bfloat16 [1024, 16], P(('dp', 'seq')), may hold values from -0.1875 to 0.1875
Outputs:
- output: bfloat16 [16, 4096, 2048], P('dp', 'seq')
- grad_pre: bfloat16 [16, 4096, 2048], P('dp', 'seq')
- grad_post: bfloat16 [16, 4096, 2048], P('dp', 'seq')
- grad_values: bfloat16 [16, 4096, 2048], P('dp', 'seq')
- grad_filters: float32 [1024, 16], P(('dp', 'seq'))
The draws below stay inside these ranges and needn't reach their ends.
All inputs are finite; a program needn't handle non-finite values.
Results may differ from the reference program's by a relative error of at most 0.005.
Values may be sent and summed in bfloat16 or wider, within the bound.
A program may use at most 128 MiB of HBM per device.

```python
import jax
import jax.numpy as jnp
from jax import lax

D = 2048
GS = 128
K = 1024
G = 16
SEQS = 16
LEN = 4096


def steps_of(own_key, dims, split, low, high):
    factor_of, own = 1.0, jax.random.fold_in(own_key, 6)
    for dim, blocks in split:
        heights = jnp.exp(jax.random.uniform(jax.random.fold_in(own, dim), (blocks,), jnp.float32, low / len(split), high / len(split)))
        factor_of = factor_of * jnp.repeat(heights, dims[dim] // blocks).reshape([-1 if axis == dim else 1 for axis in range(len(dims))])
    return factor_of


def scatter_about(stream_key, shape, deviation, most, cuts=(), dtype=jnp.bfloat16):
    values = deviation * jax.random.normal(stream_key, shape, jnp.float32)
    if cuts:
        values = values * steps_of(stream_key, shape, cuts, -0.22, 0.18)
    return jnp.clip(values, -most, most).astype(dtype)


def setup_inputs(seed: int = 0) -> dict:
    key_list = jax.random.split(jax.random.key(seed), 6)
    pre_gate = scatter_about(key_list[0], (SEQS, LEN, D), 1.0, 6.0, ((0, 16), (1, 32)))
    post_gate = scatter_about(key_list[1], (SEQS, LEN, D), 1.0, 6.0, ((0, 16), (1, 32)))
    values = scatter_about(key_list[2], (SEQS, LEN, D), 1.0, 6.0, ((0, 16), (1, 32)))
    cotangent = scatter_about(key_list[3], (SEQS, LEN, D), 1.0, 6.0, ((0, 16), (1, 32)))
    filters = scatter_about(key_list[4], (K, G), K ** -0.5, 0.1875, ((0, 512),))
    return {"pre_gate": pre_gate, "post_gate": post_gate, "values": values, "cotangent": cotangent, "filters": filters}


def reference(pre_gate, post_gate, values, cotangent, filters):
    length = LEN + K
    expanded = jnp.repeat(filters.astype(jnp.float32), GS, axis=1)
    spectrum = jnp.fft.rfft(expanded, n=length, axis=0)

    def one_sequence(items):
        pre_seq, post_seq, value_seq, cot_seq = items
        mixed_in = (pre_seq.astype(jnp.float32) * value_seq).astype(jnp.bfloat16)
        mixed_spec = jnp.fft.rfft(mixed_in.astype(jnp.float32), n=length, axis=0)
        convolved = jnp.fft.irfft(mixed_spec * spectrum, n=length, axis=0)[:LEN]
        output = (post_seq.astype(jnp.float32) * convolved).astype(jnp.bfloat16)
        grad_post = (cot_seq.astype(jnp.float32) * convolved).astype(jnp.bfloat16)
        gated = (cot_seq.astype(jnp.float32) * post_seq).astype(jnp.bfloat16)
        gated_spec = jnp.fft.rfft(gated.astype(jnp.float32), n=length, axis=0)
        carried = jnp.fft.irfft(gated_spec * jnp.conj(spectrum), n=length, axis=0)[:LEN]
        grad_pre = (carried * value_seq).astype(jnp.bfloat16)
        grad_values = (carried * pre_seq).astype(jnp.bfloat16)
        lagged = jnp.fft.irfft(gated_spec * jnp.conj(mixed_spec), n=length, axis=0)[:K]
        grouped = jnp.sum(lagged.reshape(K, G, GS), axis=2)
        return output, grad_pre, grad_post, grad_values, grouped

    output, grad_pre, grad_post, grad_values, grouped = lax.map(one_sequence, (pre_gate, post_gate, values, cotangent))
    grad_filters = jnp.sum(grouped, axis=0) / float((SEQS * LEN * GS) ** 0.5)
    return output, grad_pre, grad_post, grad_values, grad_filters
```

```python
import functools

import jax
import jax.numpy as jnp
from jax import lax
from jax.experimental import pallas as pl
from jax.experimental.pallas import tpu as pltpu
from jax.sharding import PartitionSpec as P

K = 1024
B = 128
Y = 4
REACH = K + B
MESH = pl.DeviceIdType.MESH
F32 = jnp.float32
BF16 = jnp.bfloat16


def kernel(
    dp_count, z_count,
    u_ref, pre_ref, post_ref, val_ref, cot_ref,
    r_ref, gout_ref,
    w, s, o, strips, taps, fy, fz, fd, gl, rd, rz, ry,
    yi_s, yi_r, zs_s, zs_r, yo_s, yo_r,
    fy_s, fy_r, fz_s, fz_r, fd_s, fd_r, gd_s, gd_r, gz_s, gz_r, gy_s, gy_r,
):
    dp = lax.axis_index("dp")
    seq = lax.axis_index("seq")
    z, y = seq // Y, seq % Y
    rows = Y * B

    def y_peer(d):
        return lax.rem(y + d, Y)

    def z_peer(d):
        return lax.rem(z + d, z_count)

    def dp_peer(d):
        return lax.rem(dp + d, dp_count)

    def at(z_to, y_to):
        return {"dp": dp, "seq": z_to * Y + y_to}

    barrier = pltpu.get_barrier_semaphore()

    def greet(device):
        pl.semaphore_signal(barrier, inc=1, device_id=device, device_id_type=MESH)

    for d in range(1, Y):
        greet(at(z, y_peer(d)))

    @pl.loop(1, z_count)
    def _(d):
        greet(at(z_peer(d), y))

    @pl.loop(1, dp_count)
    def _(d):
        greet({"dp": dp_peer(d), "seq": seq})

    def remote(src, dst, send, recv, device):
        return pltpu.make_async_remote_copy(
            src_ref=src, dst_ref=dst, send_sem=send, recv_sem=recv, device_id=device, device_id_type=MESH
        )

    empty = jnp.zeros((rows, B), BF16)
    for slot, outside in ((0, z < 2), (1, z < 1), (4, z > z_count - 2), (5, z > z_count - 3)):

        @pl.when(outside)
        def _(slot=slot):
            for g in range(4):
                w[g, slot] = empty

    gl[...] = jnp.zeros_like(gl)

    @pl.loop(0, 4)
    def _(g):
        for d in range(Y):
            col = pl.ds(pl.multiple_of((y_peer(d) * 4 + g) * B, B), B)
            mixed = (pre_ref[:, col].astype(F32) * val_ref[:, col].astype(F32)).astype(BF16)
            gated = (cot_ref[:, col].astype(F32) * post_ref[:, col].astype(F32)).astype(BF16)
            if d == 0:
                own = pl.ds(pl.multiple_of(y * B, B), B)
                w[g, 2, own, :] = mixed
                w[g, 3, own, :] = gated
            else:
                s[d - 1, g, 0] = mixed
                s[d - 1, g, 1] = gated

    pl.semaphore_wait(barrier, (Y - 1) + (z_count - 1) + (dp_count - 1))

    def tap_y(d):
        return remote(u_ref.at[y_peer(d)], fy.at[d - 1], fy_s.at[d - 1], fy_r.at[d - 1], at(z, y_peer(d)))

    def tap_z(d):
        return remote(fz.at[0], fz.at[d], fz_s.at[d - 1], fz_r.at[d - 1], at(z_peer(d), y))

    def tap_dp(d):
        return remote(fd.at[dp], fd.at[dp], fd_s.at[d - 1], fd_r.at[d - 1], {"dp": dp_peer(d), "seq": seq})

    def tap_dp_in(d):
        src = lax.rem(dp + dp_count - d, dp_count)
        return remote(fd.at[src], fd.at[src], fd_s.at[d - 1], fd_r.at[d - 1], {"dp": dp_peer(d), "seq": seq})

    for d in range(1, Y):
        tap_y(d).start()

    def to_owner(g, d):
        own = pl.ds(pl.multiple_of(y * B, B), B)
        return remote(
            s.at[d - 1, g], w.at[g, pl.ds(2, 2), own, :], yi_s.at[g, d - 1], yi_r.at[g, d - 1], at(z, y_peer(d))
        )

    def from_row(g, d):
        theirs = pl.ds(pl.multiple_of(lax.rem(y + Y - d, Y) * B, B), B)
        return remote(
            s.at[d - 1, g], w.at[g, pl.ds(2, 2), theirs, :], yi_s.at[g, d - 1], yi_r.at[g, d - 1], at(z, y_peer(d))
        )

    @pl.loop(0, 4)
    def _(g):
        for d in range(1, Y):
            to_owner(g, d).start()

    hops = (
        (2, 1, 1, z < z_count - 1, z >= 1),
        (3, 4, -1, z >= 1, z < z_count - 1),
        (2, 0, 2, z < z_count - 2, z >= 2),
        (3, 5, -2, z >= 2, z < z_count - 2),
    )

    def hop(g, n):
        source, target, step, _, _ = hops[n]
        to = lax.rem(z + z_count + step, z_count)
        return remote(w.at[g, source], w.at[g, target], zs_s.at[g, n], zs_r.at[g, n], at(to, y))

    def send_row(g):
        for d in range(1, Y):
            from_row(g, d).wait_recv()
        for n in range(4):

            @pl.when(hops[n][3])
            def _(n=n):
                hop(g, n).start()

    for d in range(1, Y):
        tap_y(d).wait_recv()
    fz[0] = u_ref[y] + fy[0] + fy[1] + fy[2]

    @pl.loop(1, z_count)
    def _(d):
        tap_z(d).start()

    send_row(0)

    @pl.loop(1, z_count)
    def _(d):
        tap_z(d).wait_recv()

    total = fz[0]
    for d in range(1, z_count):
        total = total + fz[d]
    fd[dp] = total

    @pl.loop(1, dp_count)
    def _(d):
        tap_dp(d).start()

    send_row(1)

    @pl.loop(1, dp_count)
    def _(d):
        tap_dp_in(d).wait_recv()

    row_id = lax.broadcasted_iota(jnp.int32, (B, B), 0)
    col_id = lax.broadcasted_iota(jnp.int32, (B, B), 1)
    flip = (row_id + col_id == B - 1).astype(BF16)
    tiles = K // B
    for j in range(tiles):
        tile = fd[2 * j] + fd[2 * j + 1]
        taps[0, :, j * B : (j + 1) * B] = tile
        k = tiles - 1 - j
        taps[1, :, k * B : (k + 1) * B] = jnp.dot(tile.astype(BF16), flip, preferred_element_type=F32)

    @pl.loop(0, 4)
    def _(g):
        tail = jnp.zeros((1, B), F32)
        for n in range(2):
            line = jnp.concatenate([taps[n, pl.ds(g, 1), :], tail], axis=1)
            wide = jnp.broadcast_to(line, (B, REACH))
            strips[g, n] = pltpu.roll(wide, n, 1, stride=1, stride_axis=0).astype(BF16)

    send_row(2)
    send_row(3)

    def give_back(g, d):
        to = y_peer(d)
        col = pl.ds(pl.multiple_of((y * 4 + g) * B, B), B)
        return remote(
            o.at[g, :, pl.ds(pl.multiple_of(to * B, B), B), :], r_ref.at[:, :, col],
            yo_s.at[g, d - 1], yo_r.at[g, d - 1], at(z, to),
        )

    def get_back(g, d):
        col = pl.ds(pl.multiple_of((lax.rem(y + Y - d, Y) * 4 + g) * B, B), B)
        return remote(
            o.at[g, :, pl.ds(pl.multiple_of(y_peer(d) * B, B), B), :], r_ref.at[:, :, col],
            yo_s.at[g, d - 1], yo_r.at[g, d - 1], at(z, y_peer(d)),
        )

    @pl.loop(0, 4)
    def _(g):
        for n in range(4):

            @pl.when(hops[n][4])
            def _(n=n):
                hop(g, n).wait_recv()

        def windows(first):
            a, b, c = w[g, first], w[g, first + 1], w[g, first + 2]
            return [jnp.concatenate([a[i * B :], b, c[: (i + 1) * B]], axis=0) for i in range(Y)]

        earlier, later = windows(0), windows(3)
        for i in range(Y):
            block = slice(i * B, (i + 1) * B)
            o[g, 0, block, :] = jnp.dot(strips[g, 1], earlier[i], preferred_element_type=F32).astype(BF16)
            o[g, 1, block, :] = jnp.dot(strips[g, 0], later[i], preferred_element_type=F32).astype(BF16)
        for d in range(1, Y):
            give_back(g, d).start()
        own = pl.ds(pl.multiple_of(y * B, B), B)
        col = pl.ds(pl.multiple_of((y * 4 + g) * B, B), B)
        for n in range(2):
            r_ref[n, :, col] = o[g, n, own, :]

        mixed = w[g, 2]
        across = jnp.concatenate([mixed[i * B : (i + 1) * B] for i in range(Y)], axis=1)
        turned = jnp.dot(flip, across, preferred_element_type=F32).astype(BF16)
        pairs = lax.dot_general(
            turned, jnp.concatenate(later, axis=1), (((1,), (1,)), ((), ())), preferred_element_type=F32
        )
        lined = pltpu.roll(pairs, REACH - (B - 1), 1, stride=1, stride_axis=0)
        gl[pl.ds(g, 1), :] = jnp.sum(lined, axis=0, keepdims=True)[:, :K]

    def tile_of(owner):
        return gl.at[:, pl.ds(pl.multiple_of(owner // 2 * B, B), B)]

    def sum_dp(d):
        to = dp_peer(d)
        return remote(tile_of(to), rd.at[d - 1], gd_s.at[d - 1], gd_r.at[d - 1], {"dp": to, "seq": seq})

    def sum_z(d):
        return remote(rz.at[0], rz.at[d], gz_s.at[d - 1], gz_r.at[d - 1], at(z_peer(d), y))

    def sum_y(d):
        return remote(ry.at[y], ry.at[y], gy_s.at[d - 1], gy_r.at[d - 1], at(z, y_peer(d)))

    def sum_y_in(d):
        src = lax.rem(y + Y - d, Y)
        return remote(ry.at[src], ry.at[src], gy_s.at[d - 1], gy_r.at[d - 1], at(z, y_peer(d)))

    @pl.loop(1, dp_count)
    def _(d):
        sum_dp(d).start()

    @pl.loop(1, dp_count)
    def _(d):
        sum_dp(d).wait_recv()

    total = gl[:, pl.ds(pl.multiple_of(dp // 2 * B, B), B)]
    for d in range(1, dp_count):
        total = total + rd[d - 1]
    rz[0] = total

    @pl.loop(1, z_count)
    def _(d):
        sum_z(d).start()

    @pl.loop(1, z_count)
    def _(d):
        sum_z(d).wait_recv()

    total = rz[0]
    for d in range(1, z_count):
        total = total + rz[d]
    ry[y] = total

    for d in range(1, Y):
        sum_y(d).start()
    for d in range(1, Y):
        sum_y_in(d).wait_recv()
    gout_ref[...] = ry[...]

    @pl.loop(0, 4)
    def _(g):
        for d in range(1, Y):
            get_back(g, d).wait_recv()
            give_back(g, d).wait_send()
            to_owner(g, d).wait_send()
        for n in range(4):

            @pl.when(hops[n][3])
            def _(n=n):
                hop(g, n).wait_send()

    for d in range(1, Y):
        tap_y(d).wait_send()
        sum_y(d).wait_send()

    @pl.loop(1, z_count)
    def _(d):
        tap_z(d).wait_send()
        sum_z(d).wait_send()

    @pl.loop(1, dp_count)
    def _(d):
        tap_dp(d).wait_send()
        sum_dp(d).wait_send()


def shards(pre_gate, post_gate, values, cotangent, filters):
    shard_len, channels = pre_gate.shape[1:]
    groups = filters.shape[1]
    dp_count, seq_count = lax.axis_size("dp"), lax.axis_size("seq")
    z_count = seq_count // Y
    dp, seq = lax.axis_index("dp"), lax.axis_index("seq")
    quarter = groups // Y
    rows = Y * B
    half = (dp % 2) * (B // 2) + 2 * seq

    lane = lax.broadcasted_iota(jnp.int32, (Y, 8, B), 2)
    mine = jnp.pad(filters.astype(F32).reshape(2, Y, quarter), ((0, 0), (0, 0), (0, 8 - quarter)))
    placed = jnp.where(lane == half, mine[0][:, :, None], 0.0) + jnp.where(lane == half + 1, mine[1][:, :, None], 0.0)

    vmem = pl.BlockSpec(memory_space=pltpu.VMEM)
    dma = pltpu.SemaphoreType.DMA
    reached, sums = pl.pallas_call(
        functools.partial(kernel, dp_count, z_count),
        name="hyena",
        out_shape=(
            jax.ShapeDtypeStruct((2, shard_len, channels), BF16),
            jax.ShapeDtypeStruct((Y, 8, B), F32),
        ),
        in_specs=[vmem] * 5,
        out_specs=(vmem, vmem),
        scratch_shapes=[
            pltpu.VMEM((4, 6, rows, B), BF16),
            pltpu.VMEM((Y - 1, 4, 2, B, B), BF16),
            pltpu.VMEM((4, 2, rows, B), BF16),
            pltpu.VMEM((4, 2, B, REACH), BF16),
            pltpu.VMEM((2, 8, K), F32),
            pltpu.VMEM((Y - 1, 8, B), F32),
            pltpu.VMEM((z_count, 8, B), F32),
            pltpu.VMEM((dp_count, 8, B), F32),
            pltpu.VMEM((8, K), F32),
            pltpu.VMEM((dp_count - 1, 8, B), F32),
            pltpu.VMEM((z_count, 8, B), F32),
            pltpu.VMEM((Y, 8, B), F32),
            dma((4, Y - 1)), dma((4, Y - 1)),
            dma((4, 4)), dma((4, 4)),
            dma((4, Y - 1)), dma((4, Y - 1)),
            dma((Y - 1,)), dma((Y - 1,)),
            dma((z_count - 1,)), dma((z_count - 1,)),
            dma((dp_count - 1,)), dma((dp_count - 1,)),
            dma((dp_count - 1,)), dma((dp_count - 1,)),
            dma((z_count - 1,)), dma((z_count - 1,)),
            dma((Y - 1,)), dma((Y - 1,)),
        ],
        compiler_params=pltpu.CompilerParams(
            collective_id=0, has_side_effects=True, vmem_limit_bytes=40 << 20
        ),
        cost_estimate=pl.CostEstimate(flops=2 * 10**9, bytes_accessed=4 << 20, transcendentals=0),
    )(placed, pre_gate[0], post_gate[0], values[0], cotangent[0])

    convolved, carried = reached[0].astype(F32), reached[1].astype(F32)
    output = (post_gate[0].astype(F32) * convolved).astype(BF16)
    grad_post = (cotangent[0].astype(F32) * convolved).astype(BF16)
    grad_pre = (carried * values[0]).astype(BF16)
    grad_values = (carried * pre_gate[0]).astype(BF16)
    owned = lax.dynamic_slice(sums[:, :quarter], (0, 0, half), (Y, quarter, 2)).reshape(groups, 2).T
    total_tokens = dp_count * shard_len * seq_count * (channels // groups)
    grad_filters = owned / float(total_tokens**0.5)
    return (output[None], grad_pre[None], grad_post[None], grad_values[None], grad_filters)


def solution(mesh):
    wide = P("dp", "seq", None)
    narrow = P(("dp", "seq"), None)
    return jax.shard_map(
        shards,
        mesh=mesh,
        in_specs=(wide, wide, wide, wide, narrow),
        out_specs=(wide, wide, wide, wide, narrow),
        check_vma=False,
    )
```

```python
import functools

import jax
import jax.numpy as jnp
from jax import lax
from jax.experimental import pallas as pl
from jax.experimental.pallas import tpu as pltpu
from jax.sharding import PartitionSpec as P

K = 1024
B = 128
Y = 4
RING = 16
REACH = K + B
DEPTH = 1
MESH = pl.DeviceIdType.MESH
F32 = jnp.float32
BF16 = jnp.bfloat16


def kernel(
    x_count, z_count, scale,
    f_hbm, pre_hbm, post_hbm, val_hbm, cot_hbm,
    r_ref, gout_ref,
    fin, wide, f_in, placed, w, s, o, strips, taps, ta, tb, gp, sb, sa,
    in_sem, yi_s, yi_r, zs_s, zs_r, yo_s, yo_r,
    ta_s, ta_r, tb_s, tb_r, sb_s, sb_r, sa_s, sa_r,
):
    dp = lax.axis_index("dp")
    seq = lax.axis_index("seq")
    z, y = seq // Y, seq % Y
    half, x, core = dp // (2 * x_count), dp // 2 % x_count, dp % 2
    rows = Y * B
    crowd = x_count * z_count

    def device(half_to, x_to, core_to, z_to, y_to):
        return {"dp": (half_to * x_count + x_to) * 2 + core_to, "seq": z_to * Y + y_to}

    def y_peer(d):
        return lax.rem(y + d, Y)

    def at(z_to, y_to):
        return {"dp": dp, "seq": z_to * Y + y_to}

    def ring_peer(e, sign=1):
        other = e // Y
        return lax.rem(half + other // 2, 2), lax.rem(core + other % 2, 2), lax.rem(y + Y + sign * (e % Y), Y)

    def ring_device(e):
        half_to, core_to, y_to = ring_peer(e)
        return device(half_to, x, core_to, z, y_to)

    def crowd_peer(e, sign=1):
        return (
            lax.rem(x + x_count + sign * (e // z_count), x_count),
            lax.rem(z + z_count + sign * (e % z_count), z_count),
        )

    def crowd_device(e):
        x_to, z_to = crowd_peer(e)
        return device(half, x_to, core, z_to, y)

    loads = [pltpu.make_async_copy(f_hbm, fin, in_sem.at[4])]
    for n, ref in enumerate((pre_hbm, val_hbm, cot_hbm, post_hbm)):
        loads.append(pltpu.make_async_copy(ref, wide.at[n], in_sem.at[n]))
    for load in loads:
        load.start()

    barrier = pltpu.get_barrier_semaphore()

    @pl.loop(1, RING)
    def _(e):
        pl.semaphore_signal(barrier, inc=1, device_id=ring_device(e), device_id_type=MESH)

    @pl.loop(1, crowd)
    def _(e):
        pl.semaphore_signal(barrier, inc=1, device_id=crowd_device(e), device_id_type=MESH)

    def remote(src, dst, send, recv, to):
        return pltpu.make_async_remote_copy(
            src_ref=src, dst_ref=dst, send_sem=send, recv_sem=recv, device_id=to, device_id_type=MESH
        )

    empty = jnp.zeros((rows, B), BF16)
    for slot, outside in ((0, z < 2), (1, z < 1), (4, z > z_count - 2), (5, z > z_count - 3)):

        @pl.when(outside)
        def _(slot=slot):
            for g in range(4):
                w[g, slot] = empty

    row_id = lax.broadcasted_iota(jnp.int32, (B, B), 0)
    col_id = lax.broadcasted_iota(jnp.int32, (B, B), 1)
    flip = (row_id + col_id == B - 1).astype(BF16)
    first_lane = core * (B // 2) + 2 * seq

    def products(g):
        for d in range(Y):
            col = pl.ds(pl.multiple_of((y_peer(d) * 4 + g) * B, B), B)
            mixed = (wide[0, :, col].astype(F32) * wide[1, :, col].astype(F32)).astype(BF16)
            gated = (wide[2, :, col].astype(F32) * wide[3, :, col].astype(F32)).astype(BF16)
            if d == 0:
                own = pl.ds(pl.multiple_of(y * B, B), B)
                w[g, 2, own, :] = mixed
                w[g, 3, own, :] = gated
            else:
                s[d - 1, g, 0] = mixed
                s[d - 1, g, 1] = gated

    def to_owner(g, d):
        own = pl.ds(pl.multiple_of(y * B, B), B)
        return remote(
            s.at[d - 1, g], w.at[g, pl.ds(2, 2), own, :], yi_s.at[g, d - 1], yi_r.at[g, d - 1], at(z, y_peer(d))
        )

    def from_row(g, d):
        theirs = pl.ds(pl.multiple_of(lax.rem(y + Y - d, Y) * B, B), B)
        return remote(
            s.at[d - 1, g], w.at[g, pl.ds(2, 2), theirs, :], yi_s.at[g, d - 1], yi_r.at[g, d - 1], at(z, y_peer(d))
        )

    def row_start(g):
        for d in range(1, Y):
            to_owner(g, d).start()

    def row_sent(g):
        for d in range(1, Y):
            to_owner(g, d).wait_send()

    def row_arrive(g):
        for d in range(1, Y):
            from_row(g, d).wait_recv()

    inner = (z >= 1) & (z < z_count - 1)
    hops = (
        ((2, 1, 1, z < z_count - 1, z >= 1), (3, 4, -1, z >= 1, z < z_count - 1)),
        ((1, 0, 1, inner, z >= 2), (4, 5, -1, inner, z < z_count - 2)),
    )

    def hop(g, turn, n):
        source, target, step, _, _ = hops[turn][n]
        to = lax.rem(z + z_count + step, z_count)
        sem = 2 * turn + n
        return remote(w.at[g, source], w.at[g, target], zs_s.at[g, sem], zs_r.at[g, sem], at(to, y))

    def hop_start(g, turn):
        for n in range(2):

            @pl.when(hops[turn][n][3])
            def _(n=n):
                hop(g, turn, n).start()

    def hop_arrive(g, turn):
        for n in range(2):

            @pl.when(hops[turn][n][4])
            def _(n=n):
                hop(g, turn, n).wait_recv()

    def tap_ring(e):
        _, _, y_to = ring_peer(e)
        return remote(placed.at[y_to], ta.at[e], ta_s.at[e - 1], ta_r.at[e - 1], ring_device(e))

    def tap_crowd(e):
        here = x * z_count + z
        return remote(tb.at[here], tb.at[here], tb_s.at[e - 1], tb_r.at[e - 1], crowd_device(e))

    def tap_crowd_in(e):
        x_from, z_from = crowd_peer(e, -1)
        there = x_from * z_count + z_from
        return remote(tb.at[there], tb.at[there], tb_s.at[e - 1], tb_r.at[e - 1], crowd_device(e))

    for load in loads[1:]:
        load.wait()
    products(0)
    pl.semaphore_wait(barrier, (RING - 1) + (crowd - 1))
    row_start(0)

    f_in[...] = jnp.zeros_like(f_in)
    loads[0].wait()
    f_in[0:2, 0 : 4 * Y] = fin[...]
    r16 = lax.broadcasted_iota(jnp.int32, (16, B), 0)
    c16 = lax.broadcasted_iota(jnp.int32, (16, B), 1)
    lane_of = ((c16 == first_lane + r16) & (r16 < 2)).astype(BF16)
    by_group = lax.dot_general(f_in[...], lane_of, (((0,), (0,)), ((), ())), preferred_element_type=F32)
    r32 = lax.broadcasted_iota(jnp.int32, (8 * Y, B), 0)
    c32 = lax.broadcasted_iota(jnp.int32, (8 * Y, B), 1)
    group_of = (c32 == r32 // 8 * 4 + r32 % 4) & (r32 % 8 // 4 == half)
    spots = jnp.dot(group_of.astype(BF16), by_group.astype(BF16), preferred_element_type=F32)
    for q in range(Y):
        placed[q] = spots[q * 8 : q * 8 + 8]
    ta[0] = placed[y]

    @pl.loop(1, RING)
    def _(e):
        tap_ring(e).start()

    for g in range(1, 4):
        products(g)
        if g < DEPTH:
            row_start(g)

    def turn_row(t):
        row_sent(t - DEPTH)
        row_start(t)

    for t in range(DEPTH, 2):
        turn_row(t)
    row_arrive(0)
    hop_start(0, 0)

    @pl.loop(1, RING)
    def _(e):
        tap_ring(e).wait_recv()

    total = ta[0]
    for e in range(1, RING):
        total = total + ta[e]
    tb[x * z_count + z] = total

    @pl.loop(1, crowd)
    def _(e):
        tap_crowd(e).start()

    turn_row(2)
    row_arrive(1)
    hop_start(1, 0)
    hop_arrive(0, 0)
    hop_start(0, 1)

    @pl.loop(1, crowd)
    def _(e):
        tap_crowd_in(e).wait_recv()

    tiles = K // B
    for n in range(x_count):
        total = tb[n * z_count]
        for m in range(1, z_count):
            total = total + tb[n * z_count + m]
        turned = jnp.dot(total.astype(BF16), flip, preferred_element_type=F32)
        for m in range(2):
            j = m * x_count + n
            k = tiles - 1 - j
            taps[0, 0:4, j * B : (j + 1) * B] = total[m * 4 : m * 4 + 4]
            taps[1, 0:4, k * B : (k + 1) * B] = turned[m * 4 : m * 4 + 4]

    @pl.loop(0, 4)
    def _(g):
        tail = jnp.zeros((1, B), F32)
        for n in range(2):
            line = jnp.concatenate([taps[n, pl.ds(g, 1), :], tail], axis=1)
            spread = jnp.broadcast_to(line, (B, REACH))
            strips[g, n] = pltpu.roll(spread, n, 1, stride=1, stride_axis=0).astype(BF16)

    def give_back(g, d):
        to = y_peer(d)
        col = pl.ds(pl.multiple_of((y * 4 + g) * B, B), B)
        return remote(
            o.at[g, :, pl.ds(pl.multiple_of(to * B, B), B), :], r_ref.at[:, :, col],
            yo_s.at[g, d - 1], yo_r.at[g, d - 1], at(z, to),
        )

    def get_back(g, d):
        col = pl.ds(pl.multiple_of((lax.rem(y + Y - d, Y) * 4 + g) * B, B), B)
        return remote(
            o.at[g, :, pl.ds(pl.multiple_of(y_peer(d) * B, B), B), :], r_ref.at[:, :, col],
            yo_s.at[g, d - 1], yo_r.at[g, d - 1], at(z, y_peer(d)),
        )

    def sum_crowd(e):
        x_to, _ = crowd_peer(e)
        return remote(gp.at[x_to], sb.at[e - 1], sb_s.at[e - 1], sb_r.at[e - 1], crowd_device(e))

    def sum_ring(e):
        here = y * Y + half * 2 + core
        return remote(sa.at[here], sa.at[here], sa_s.at[e - 1], sa_r.at[e - 1], ring_device(e))

    def sum_ring_in(e):
        half_from, core_from, y_from = ring_peer(e, -1)
        there = y_from * Y + half_from * 2 + core_from
        return remote(sa.at[there], sa.at[there], sa_s.at[e - 1], sa_r.at[e - 1], ring_device(e))

    def finish(g):
        def windows(first):
            a, b, c = w[g, first], w[g, first + 1], w[g, first + 2]
            return [jnp.concatenate([a[i * B :], b, c[: (i + 1) * B]], axis=0) for i in range(Y)]

        earlier, later = windows(0), windows(3)
        mixed = w[g, 2]
        across = jnp.concatenate([mixed[i * B : (i + 1) * B] for i in range(Y)], axis=1)
        turned = jnp.dot(flip, across, preferred_element_type=F32).astype(BF16)
        pairs = lax.dot_general(
            turned, jnp.concatenate(later, axis=1), (((1,), (1,)), ((), ())), preferred_element_type=F32
        )
        lined = pltpu.roll(pairs, REACH - (B - 1), 1, stride=1, stride_axis=0)
        lags = jnp.sum(lined, axis=0, keepdims=True)
        for j in range(tiles):
            gp[j % x_count, pl.ds(j // x_count * 4 + g, 1), :] = lags[:, j * B : (j + 1) * B]

        @pl.when(g == 3)
        def _():
            @pl.loop(1, crowd)
            def _(e):
                sum_crowd(e).start()

        for i in range(Y):
            block = slice(i * B, (i + 1) * B)
            o[g, 0, block, :] = jnp.dot(strips[g, 1], earlier[i], preferred_element_type=F32).astype(BF16)
            o[g, 1, block, :] = jnp.dot(strips[g, 0], later[i], preferred_element_type=F32).astype(BF16)
        for d in range(1, Y):
            give_back(g, d).start()
        own = pl.ds(pl.multiple_of(y * B, B), B)
        col = pl.ds(pl.multiple_of((y * 4 + g) * B, B), B)
        for n in range(2):
            r_ref[n, :, col] = o[g, n, own, :]

    @pl.loop(3, 7)
    def _(t):
        @pl.when(t < 4)
        def _():
            turn_row(t)

        @pl.when(t < 5)
        def _():
            row_arrive(t - 1)
            hop_start(t - 1, 0)

        @pl.when(t < 6)
        def _():
            hop_arrive(t - 2, 0)
            hop_start(t - 2, 1)

        hop_arrive(t - 3, 1)
        finish(t - 3)

    @pl.loop(1, crowd)
    def _(e):
        sum_crowd(e).wait_recv()

    total = gp[x]
    for e in range(1, crowd):
        total = total + sb[e - 1]
    sa[y * Y + half * 2 + core] = total

    @pl.loop(1, RING)
    def _(e):
        sum_ring(e).start()

    @pl.loop(1, RING)
    def _(e):
        sum_ring_in(e).wait_recv()

    mine = []
    for q in range(Y):
        total = sa[q * Y]
        for n in range(1, Y):
            total = total + sa[q * Y + n]
        mine.append(jnp.where(half == 0, total[0:4], total[4:8]))
    hit = lax.broadcasted_iota(jnp.int32, (8, B), 1) == first_lane + lax.broadcasted_iota(jnp.int32, (8, B), 0)
    picked = lax.dot_general(
        hit.astype(F32), jnp.concatenate(mine, axis=0), (((1,), (1,)), ((), ())),
        precision=lax.Precision.HIGHEST, preferred_element_type=F32,
    )
    gout_ref[...] = picked[0:2] / scale

    @pl.loop(0, 4)
    def _(g):
        for d in range(1, Y):
            get_back(g, d).wait_recv()
            give_back(g, d).wait_send()
        for turn in range(2):
            for n in range(2):

                @pl.when(hops[turn][n][3])
                def _(turn=turn, n=n):
                    hop(g, turn, n).wait_send()

    for g in range(4 - DEPTH, 4):
        row_sent(g)

    @pl.loop(1, RING)
    def _(e):
        tap_ring(e).wait_send()
        sum_ring(e).wait_send()

    @pl.loop(1, crowd)
    def _(e):
        tap_crowd(e).wait_send()
        sum_crowd(e).wait_send()


def shards(pre_gate, post_gate, values, cotangent, filters):
    shard_len, channels = pre_gate.shape[1:]
    groups = filters.shape[1]
    dp_count, seq_count = lax.axis_size("dp"), lax.axis_size("seq")
    z_count, x_count = seq_count // Y, dp_count * Y // RING
    crowd = x_count * z_count
    rows = Y * B
    total_tokens = dp_count * shard_len * seq_count * (channels // groups)

    vmem = pl.BlockSpec(memory_space=pltpu.VMEM)
    hbm = pl.BlockSpec(memory_space=pltpu.HBM)
    dma = pltpu.SemaphoreType.DMA
    operands = (filters, pre_gate[0], post_gate[0], values[0], cotangent[0])
    reached, grad_filters = pl.pallas_call(
        functools.partial(kernel, x_count, z_count, float(total_tokens**0.5)),
        name="hyena",
        out_shape=(
            jax.ShapeDtypeStruct((2, shard_len, channels), BF16),
            jax.ShapeDtypeStruct((2, groups), F32),
        ),
        in_specs=[hbm] * 5,
        out_specs=(vmem, vmem),
        scratch_shapes=[
            pltpu.VMEM((2, groups), BF16),
            pltpu.VMEM((4, shard_len, channels), BF16),
            pltpu.VMEM((16, B), BF16),
            pltpu.VMEM((Y, 8, B), F32),
            pltpu.VMEM((4, 6, rows, B), BF16),
            pltpu.VMEM((Y - 1, 4, 2, B, B), BF16),
            pltpu.VMEM((4, 2, rows, B), BF16),
            pltpu.VMEM((4, 2, B, REACH), BF16),
            pltpu.VMEM((2, 8, K), F32),
            pltpu.VMEM((RING, 8, B), F32),
            pltpu.VMEM((crowd, 8, B), F32),
            pltpu.VMEM((x_count, 8, B), F32),
            pltpu.VMEM((crowd - 1, 8, B), F32),
            pltpu.VMEM((RING, 8, B), F32),
            dma((5,)),
            dma((4, Y - 1)), dma((4, Y - 1)),
            dma((4, 4)), dma((4, 4)),
            dma((4, Y - 1)), dma((4, Y - 1)),
            dma((RING - 1,)), dma((RING - 1,)),
            dma((crowd - 1,)), dma((crowd - 1,)),
            dma((crowd - 1,)), dma((crowd - 1,)),
            dma((RING - 1,)), dma((RING - 1,)),
        ],
        compiler_params=pltpu.CompilerParams(
            collective_id=0, has_side_effects=True, vmem_limit_bytes=40 << 20
        ),
        cost_estimate=pl.CostEstimate(flops=2 * 10**9, bytes_accessed=4 << 20, transcendentals=0),
    )(*(pltpu.with_memory_space_constraint(operand, pltpu.HBM) for operand in operands))

    convolved, carried = reached[0].astype(F32), reached[1].astype(F32)
    output = (post_gate[0].astype(F32) * convolved).astype(BF16)
    grad_post = (cotangent[0].astype(F32) * convolved).astype(BF16)
    grad_pre = (carried * values[0]).astype(BF16)
    grad_values = (carried * pre_gate[0]).astype(BF16)
    return (output[None], grad_pre[None], grad_post[None], grad_values[None], grad_filters)


def solution(mesh):
    wide = P("dp", "seq", None)
    narrow = P(("dp", "seq"), None)
    return jax.shard_map(
        shards,
        mesh=mesh,
        in_specs=(wide, wide, wide, wide, narrow),
        out_specs=(wide, wide, wide, wide, narrow),
        check_vma=False,
    )
```

```python
import functools

import jax
import jax.numpy as jnp
from jax import lax
from jax.experimental import pallas as pl
from jax.experimental.pallas import tpu as pltpu
from jax.sharding import PartitionSpec as P

K = 1024
B = 128
Y = 4
RING = 16
REACH = K + B
PIECES = 8
DEPTH = 1
HELD = 6
MESH = pl.DeviceIdType.MESH
F32 = jnp.float32
BF16 = jnp.bfloat16


def kernel(
    x_count, z_count, scale,
    f_hbm, pre_hbm, post_hbm, val_hbm, cot_hbm,
    r_ref, gout_ref,
    fin, wide, f_in, placed, w, s, o, strips, taps, ta, tb, gp, sb, sa,
    in_sem, yi_s, yi_r, zs_s, zs_r, yo_s, yo_r,
    ta_s, ta_r, tb_s, tb_r, sb_s, sb_r, sa_s, sa_r,
):
    dp = lax.axis_index("dp")
    seq = lax.axis_index("seq")
    z, y = seq // Y, seq % Y
    half, x, core = dp // (2 * x_count), dp // 2 % x_count, dp % 2
    rows = Y * B
    crowd = x_count * z_count

    def device(half_to, x_to, core_to, z_to, y_to):
        return {"dp": (half_to * x_count + x_to) * 2 + core_to, "seq": z_to * Y + y_to}

    xs = [lax.rem(x + d, x_count) for d in range(x_count)]
    zs = [lax.rem(z + d, z_count) for d in range(z_count)]
    ys = [lax.rem(y + d, Y) for d in range(Y)]
    halves, cores = (half, 1 - half), (core, 1 - core)

    def y_peer(d):
        return ys[d]

    def at(z_to, y_to):
        return {"dp": dp, "seq": z_to * Y + y_to}

    def ring_device(e):
        return device(halves[e // Y // 2], x, cores[e // Y % 2], z, ys[e % Y])

    def crowd_device(e):
        return device(half, xs[e // z_count], core, zs[e % z_count], y)

    near = at(z, ys[1])

    loads = [pltpu.make_async_copy(f_hbm, fin, in_sem.at[4])]
    for n, ref in enumerate((cot_hbm, post_hbm, pre_hbm, val_hbm)):
        loads.append(pltpu.make_async_copy(ref, wide.at[n], in_sem.at[n]))
    for load in loads:
        load.start()

    barrier = pltpu.get_barrier_semaphore()

    for e in range(1, RING):
        pl.semaphore_signal(barrier, inc=1, device_id=ring_device(e), device_id_type=MESH)
    for e in range(1, crowd):
        pl.semaphore_signal(barrier, inc=1, device_id=crowd_device(e), device_id_type=MESH)

    def remote(src, dst, send, recv, to):
        return pltpu.make_async_remote_copy(
            src_ref=src, dst_ref=dst, send_sem=send, recv_sem=recv, device_id=to, device_id_type=MESH
        )

    empty = jnp.zeros((rows, B), BF16)
    for slot, outside in ((0, z < 2), (1, z < 1), (4, z > z_count - 2), (5, z > z_count - 3)):

        @pl.when(outside)
        def _(slot=slot):
            for g in range(4):
                w[g, slot] = empty

    row_id = lax.broadcasted_iota(jnp.int32, (B, B), 0)
    col_id = lax.broadcasted_iota(jnp.int32, (B, B), 1)
    flip = (row_id + col_id == B - 1).astype(BF16)
    first_lane = core * (B // 2) + 2 * seq

    def piece(i):
        last = lax.div(i, PIECES - 1)
        kind = lax.rem(i, 2) * (1 - last) + 1 - lax.div(i + PIECES - 1, PIECES)
        return kind, lax.div(i + 1, 2) - 1 + kind

    def products(i):
        kind, g = piece(i)
        for d in range(Y):
            col = pl.ds(pl.multiple_of((y_peer(d) * 4 + g) * B, B), B)
            product = (wide[2 - 2 * kind, :, col].astype(F32) * wide[3 - 2 * kind, :, col].astype(F32)).astype(BF16)
            if d == 0:
                w[g, 2 + kind, pl.ds(pl.multiple_of(y * B, B), B), :] = product
            else:
                s[d - 1, i] = product

    def to_owner(i, d):
        kind, g = piece(i)
        own = pl.ds(pl.multiple_of(y * B, B), B)
        return remote(
            s.at[d - 1, i], w.at[g, 2 + kind, own, :], yi_s.at[i, d - 1], yi_r.at[i, d - 1], at(z, y_peer(d))
        )

    def from_row(i, d):
        kind, g = piece(i)
        theirs = pl.ds(pl.multiple_of(lax.rem(y + Y - d, Y) * B, B), B)
        return remote(
            s.at[d - 1, i], w.at[g, 2 + kind, theirs, :], yi_s.at[i, d - 1], yi_r.at[i, d - 1], at(z, y_peer(d))
        )

    def row_start(i):
        for d in range(1, Y):
            to_owner(i, d).start()

    def row_sent(i):
        for d in range(1, Y):
            to_owner(i, d).wait_send()

    def row_arrive(i):
        for d in range(1, Y):
            from_row(i, d).wait_recv()

    def hop(i, turn):
        kind, g = piece(i)
        to = lax.rem(z + z_count + 1 - 2 * kind, z_count)
        source, target = (2 + kind, 1 + 3 * kind) if turn == 0 else (1 + 3 * kind, 5 * kind)
        return remote(w.at[g, source], w.at[g, target], zs_s.at[i, turn], zs_r.at[i, turn], at(to, y))

    def depth_of(i):
        kind, _ = piece(i)
        return (1 - kind) * z + kind * (z_count - 1 - z)

    def hop_leaves(i, turn):
        return (depth_of(i) >= turn) & (depth_of(i) < z_count - 1)

    def hop_start(i, turn):
        @pl.when(hop_leaves(i, turn))
        def _():
            hop(i, turn).start()

    def hop_arrive(i, turn):
        @pl.when(depth_of(i) >= turn + 1)
        def _():
            hop(i, turn).wait_recv()

    def tap_ring(e, to=near):
        source = ys[e % Y] if isinstance(e, int) else 0
        return remote(placed.at[source], ta.at[e], ta_s.at[e - 1], ta_r.at[e - 1], to)

    def tap_crowd(e, to=near):
        return remote(tb.at[0], tb.at[e], tb_s.at[e - 1], tb_r.at[e - 1], to)

    f_in[...] = jnp.zeros_like(f_in)
    loads[0].wait()
    f_in[0:2, 0 : 4 * Y] = fin[...]
    r16 = lax.broadcasted_iota(jnp.int32, (16, B), 0)
    c16 = lax.broadcasted_iota(jnp.int32, (16, B), 1)
    lane_of = ((c16 == first_lane + r16) & (r16 < 2)).astype(BF16)
    by_group = lax.dot_general(f_in[...], lane_of, (((0,), (0,)), ((), ())), preferred_element_type=F32)
    r32 = lax.broadcasted_iota(jnp.int32, (8 * Y, B), 0)
    c32 = lax.broadcasted_iota(jnp.int32, (8 * Y, B), 1)
    group_of = (c32 == r32 // 8 * 4 + r32 % 4) & (r32 % 8 // 4 == half)
    spots = jnp.dot(group_of.astype(BF16), by_group.astype(BF16), preferred_element_type=F32)
    for q in range(Y):
        placed[q] = spots[q * 8 : q * 8 + 8]
    ta[0] = placed[y]

    loads[1].wait()
    loads[2].wait()
    products(0)
    pl.semaphore_wait(barrier, (RING - 1) + (crowd - 1))
    for e in range(1, RING):
        tap_ring(e, ring_device(e)).start()

    row_start(0)
    loads[3].wait()
    loads[4].wait()
    for i in range(1, DEPTH):
        products(i)
        row_start(i)

    @pl.loop(DEPTH, PIECES)
    def _(i):
        products(i)

    def arrive(i):
        @pl.when(i + DEPTH < PIECES)
        def _():
            row_sent(i)
            row_start(i + DEPTH)

        row_arrive(i)
        hop_start(i, 0)

    def forward(i):
        hop_arrive(i, 0)
        hop_start(i, 1)

    arrive(0)

    @pl.loop(1, RING)
    def _(e):
        tap_ring(e).wait_recv()

    total = ta[0]
    for e in range(1, RING):
        total = total + ta[e]
    tb[0] = total

    for e in range(1, crowd):
        tap_crowd(e, crowd_device(e)).start()

    arrive(1)
    arrive(2)
    forward(0)
    arrive(3)
    forward(1)

    tiles = K // B

    def build_strips():
        @pl.loop(1, crowd)
        def _(e):
            tap_crowd(e).wait_recv()

        for n in range(x_count):
            total = tb[n * z_count]
            for m in range(1, z_count):
                total = total + tb[n * z_count + m]
            turned = jnp.dot(total.astype(BF16), flip, preferred_element_type=F32)
            for m in range(2):
                j = m * x_count + xs[(x_count - n) % x_count]
                k = tiles - 1 - j
                taps[0, 0:4, pl.ds(pl.multiple_of(j * B, B), B)] = total[m * 4 : m * 4 + 4]
                taps[1, 0:4, pl.ds(pl.multiple_of(k * B, B), B)] = turned[m * 4 : m * 4 + 4]

        @pl.loop(0, 4)
        def _(g):
            tail = jnp.zeros((1, B), F32)
            for n in range(2):
                line = jnp.concatenate([taps[n, pl.ds(g, 1), :], tail], axis=1)
                spread = jnp.broadcast_to(line, (B, REACH))
                strips[g, n] = pltpu.roll(spread, n, 1, stride=1, stride_axis=0).astype(BF16)

    def give_back(i, d):
        kind, g = piece(i)
        to = y_peer(d)
        col = pl.ds(pl.multiple_of((y * 4 + g) * B, B), B)
        return remote(
            o.at[i, pl.ds(pl.multiple_of(to * B, B), B), :], r_ref.at[kind, :, col],
            yo_s.at[i, d - 1], yo_r.at[i, d - 1], at(z, to),
        )

    def get_back(i, d):
        kind, g = piece(i)
        col = pl.ds(pl.multiple_of((lax.rem(y + Y - d, Y) * 4 + g) * B, B), B)
        return remote(
            o.at[i, pl.ds(pl.multiple_of(y_peer(d) * B, B), B), :], r_ref.at[kind, :, col],
            yo_s.at[i, d - 1], yo_r.at[i, d - 1], at(z, y_peer(d)),
        )

    def sum_crowd(e, to=near):
        source = xs[e // z_count] if isinstance(e, int) else 0
        return remote(gp.at[source], sb.at[e - 1], sb_s.at[e - 1], sb_r.at[e - 1], to)

    def sum_ring(e, to=near):
        return remote(sa.at[0], sa.at[e], sa_s.at[e - 1], sa_r.at[e - 1], to)

    def windows(g, first):
        a, b, c = w[g, first], w[g, first + 1], w[g, first + 2]
        return [jnp.concatenate([a[i * B :], b, c[: (i + 1) * B]], axis=0) for i in range(Y)]

    def convolve(i, strip, reach):
        for n in range(Y):
            o[i, n * B : (n + 1) * B, :] = jnp.dot(strip, reach[n], preferred_element_type=F32).astype(BF16)

    def release(first, end):
        @pl.loop(first, end)
        def _(i):
            for d in range(1, Y):
                give_back(i, d).start()

    def correlate(i):
        kind, g = piece(i)
        hop_arrive(i, 1)

        @pl.when(kind == 1)
        def _():
            mixed = w[g, 2]
            across = jnp.concatenate([mixed[n * B : (n + 1) * B] for n in range(Y)], axis=1)
            turned = jnp.dot(flip, across, preferred_element_type=F32).astype(BF16)
            pairs = lax.dot_general(
                turned, jnp.concatenate(windows(g, 3), axis=1), (((1,), (1,)), ((), ())), preferred_element_type=F32
            )
            lined = pltpu.roll(pairs, REACH - (B - 1), 1, stride=1, stride_axis=0)
            lags = jnp.sum(lined, axis=0, keepdims=True)
            for j in range(tiles):
                gp[j % x_count, pl.ds(j // x_count * 4 + g, 1), :] = lags[:, j * B : (j + 1) * B]

            @pl.when(g == 3)
            def _():
                for e in range(1, crowd):
                    sum_crowd(e, crowd_device(e)).start()

    def finish(i):
        kind, g = piece(i)

        @pl.when(kind == 1)
        def _():
            convolve(i, strips[g, 0], windows(g, 3))

        @pl.when(kind == 0)
        def _():
            convolve(i, strips[g, 1], windows(g, 0))

        col = pl.ds(pl.multiple_of((y * 4 + g) * B, B), B)
        r_ref[kind, :, col] = o[i, pl.ds(pl.multiple_of(y * B, B), B), :]

        @pl.when(i < HELD)
        def _():
            release(i, i + 1)

    @pl.loop(4, PIECES + 4)
    def _(t):
        @pl.when(t < PIECES)
        def _():
            arrive(t)

        @pl.when(t < PIECES + 2)
        def _():
            forward(t - 2)

        correlate(t - 4)

        @pl.when(t == 6)
        def _():
            build_strips()

            @pl.loop(0, 2)
            def _(i):
                finish(i)

        @pl.when(t >= 6)
        def _():
            finish(t - 4)

    @pl.loop(1, crowd)
    def _(e):
        sum_crowd(e).wait_recv()

    total = gp[x]
    for e in range(1, crowd):
        total = total + sb[e - 1]
    sa[0] = total

    for e in range(1, RING):
        sum_ring(e, ring_device(e)).start()

    release(HELD, PIECES)

    @pl.loop(1, RING)
    def _(e):
        sum_ring(e).wait_recv()

    @pl.loop(1, RING)
    def _(e):
        tap_ring(e).wait_send()

    for d in range(Y):
        total = sa[d]
        for n in range(1, Y):
            total = total + sa[n * Y + d]
        placed[ys[(Y - d) % Y]] = total
    mine = [jnp.where(half == 0, placed[q, 0:4], placed[q, 4:8]) for q in range(Y)]
    hit = lax.broadcasted_iota(jnp.int32, (8, B), 1) == first_lane + lax.broadcasted_iota(jnp.int32, (8, B), 0)
    picked = lax.dot_general(
        hit.astype(F32), jnp.concatenate(mine, axis=0), (((1,), (1,)), ((), ())),
        precision=lax.Precision.HIGHEST, preferred_element_type=F32,
    )
    gout_ref[...] = picked[0:2] / scale

    @pl.loop(0, PIECES)
    def _(i):
        for d in range(1, Y):
            get_back(i, d).wait_recv()
            give_back(i, d).wait_send()
        for turn in range(2):

            @pl.when(hop_leaves(i, turn))
            def _(turn=turn):
                hop(i, turn).wait_send()

    for i in range(PIECES - DEPTH, PIECES):
        row_sent(i)

    @pl.loop(1, RING)
    def _(e):
        sum_ring(e).wait_send()

    @pl.loop(1, crowd)
    def _(e):
        tap_crowd(e).wait_send()
        sum_crowd(e).wait_send()


def shards(pre_gate, post_gate, values, cotangent, filters):
    shard_len, channels = pre_gate.shape[1:]
    groups = filters.shape[1]
    dp_count, seq_count = lax.axis_size("dp"), lax.axis_size("seq")
    z_count, x_count = seq_count // Y, dp_count * Y // RING
    crowd = x_count * z_count
    rows = Y * B
    total_tokens = dp_count * shard_len * seq_count * (channels // groups)

    vmem = pl.BlockSpec(memory_space=pltpu.VMEM)
    hbm = pl.BlockSpec(memory_space=pltpu.HBM)
    dma = pltpu.SemaphoreType.DMA
    operands = (filters, pre_gate[0], post_gate[0], values[0], cotangent[0])
    reached, grad_filters = pl.pallas_call(
        functools.partial(kernel, x_count, z_count, float(total_tokens**0.5)),
        name="hyena",
        out_shape=(
            jax.ShapeDtypeStruct((2, shard_len, channels), BF16),
            jax.ShapeDtypeStruct((2, groups), F32),
        ),
        in_specs=[hbm] * 5,
        out_specs=(vmem, vmem),
        scratch_shapes=[
            pltpu.VMEM((2, groups), BF16),
            pltpu.VMEM((4, shard_len, channels), BF16),
            pltpu.VMEM((16, B), BF16),
            pltpu.VMEM((Y, 8, B), F32),
            pltpu.VMEM((4, 6, rows, B), BF16),
            pltpu.VMEM((Y - 1, PIECES, B, B), BF16),
            pltpu.VMEM((PIECES, rows, B), BF16),
            pltpu.VMEM((4, 2, B, REACH), BF16),
            pltpu.VMEM((2, 8, K), F32),
            pltpu.VMEM((RING, 8, B), F32),
            pltpu.VMEM((crowd, 8, B), F32),
            pltpu.VMEM((x_count, 8, B), F32),
            pltpu.VMEM((crowd - 1, 8, B), F32),
            pltpu.VMEM((RING, 8, B), F32),
            dma((5,)),
            dma((PIECES, Y - 1)), dma((PIECES, Y - 1)),
            dma((PIECES, 2)), dma((PIECES, 2)),
            dma((PIECES, Y - 1)), dma((PIECES, Y - 1)),
            dma((RING - 1,)), dma((RING - 1,)),
            dma((crowd - 1,)), dma((crowd - 1,)),
            dma((crowd - 1,)), dma((crowd - 1,)),
            dma((RING - 1,)), dma((RING - 1,)),
        ],
        compiler_params=pltpu.CompilerParams(
            collective_id=0, has_side_effects=True, vmem_limit_bytes=40 << 20
        ),
        cost_estimate=pl.CostEstimate(flops=2 * 10**9, bytes_accessed=4 << 20, transcendentals=0),
    )(*(pltpu.with_memory_space_constraint(operand, pltpu.HBM) for operand in operands))

    convolved, carried = reached[0].astype(F32), reached[1].astype(F32)
    output = (post_gate[0].astype(F32) * convolved).astype(BF16)
    grad_post = (cotangent[0].astype(F32) * convolved).astype(BF16)
    grad_pre = (carried * values[0]).astype(BF16)
    grad_values = (carried * pre_gate[0]).astype(BF16)
    return (output[None], grad_pre[None], grad_post[None], grad_values[None], grad_filters)


def solution(mesh):
    wide = P("dp", "seq", None)
    narrow = P(("dp", "seq"), None)
    return jax.shard_map(
        shards,
        mesh=mesh,
        in_specs=(wide, wide, wide, wide, narrow),
        out_specs=(wide, wide, wide, wide, narrow),
        check_vma=False,
    )
```

```python
import functools

import jax
import jax.numpy as jnp
from jax import lax
from jax.experimental import pallas as pl
from jax.experimental.pallas import tpu as pltpu
from jax.sharding import PartitionSpec as P

K = 1024
B = 128
Y = 4
RING = 16
REACH = K + B
PIECES = 8
DEPTH = 1
HELD = 6
MESH = pl.DeviceIdType.MESH
F32 = jnp.float32
BF16 = jnp.bfloat16


def kernel(
    x_count, z_count, scale,
    f_hbm, pre_hbm, post_hbm, val_hbm, cot_hbm,
    r_ref, gout_ref,
    fin, wide, f_in, placed, w, s, o, strips, taps, ta, tb, gp, sb, sa, quarters,
    in_sem, yi_s, yi_r, zs_s, zs_r, yo_s, yo_r,
    ta_s, ta_r, tb_s, tb_r, sb_s, sb_r, sa_s, sa_r,
):
    dp = lax.axis_index("dp")
    seq = lax.axis_index("seq")
    z, y = seq // Y, seq % Y
    half, x, core = dp // (2 * x_count), dp // 2 % x_count, dp % 2
    rows = Y * B
    crowd = x_count * z_count

    def device(half_to, x_to, core_to, z_to, y_to):
        return {"dp": (half_to * x_count + x_to) * 2 + core_to, "seq": z_to * Y + y_to}

    xs = [lax.rem(x + d, x_count) for d in range(x_count)]
    zs = [lax.rem(z + d, z_count) for d in range(z_count)]
    ys = [lax.rem(y + d, Y) for d in range(Y)]
    halves, cores = (half, 1 - half), (core, 1 - core)

    def y_peer(d):
        return ys[d]

    def at(z_to, y_to):
        return {"dp": dp, "seq": z_to * Y + y_to}

    def ring_device(e):
        return device(halves[e // Y // 2], x, cores[e // Y % 2], z, ys[e % Y])

    def crowd_device(e):
        return device(half, xs[e // z_count], core, zs[e % z_count], y)

    near = at(z, ys[1])

    loads = [pltpu.make_async_copy(f_hbm, fin, in_sem.at[4])]
    for n, ref in enumerate((cot_hbm, post_hbm, pre_hbm, val_hbm)):
        loads.append(pltpu.make_async_copy(ref, wide.at[n], in_sem.at[n]))
    for load in loads:
        load.start()

    barrier = pltpu.get_barrier_semaphore()

    for e in range(1, RING):
        pl.semaphore_signal(barrier, inc=1, device_id=ring_device(e), device_id_type=MESH)
    for e in range(1, crowd):
        pl.semaphore_signal(barrier, inc=1, device_id=crowd_device(e), device_id_type=MESH)

    def remote(src, dst, send, recv, to):
        return pltpu.make_async_remote_copy(
            src_ref=src, dst_ref=dst, send_sem=send, recv_sem=recv, device_id=to, device_id_type=MESH
        )

    empty = jnp.zeros((rows, B), BF16)
    for slot, outside in ((0, z < 2), (1, z < 1), (4, z > z_count - 2), (5, z > z_count - 3)):

        @pl.when(outside)
        def _(slot=slot):
            for g in range(4):
                w[g, slot] = empty

    row_id = lax.broadcasted_iota(jnp.int32, (B, B), 0)
    col_id = lax.broadcasted_iota(jnp.int32, (B, B), 1)
    flip = (row_id + col_id == B - 1).astype(BF16)
    first_lane = core * (B // 2) + 2 * seq

    def piece(i):
        last = lax.div(i, PIECES - 1)
        kind = lax.rem(i, 2) * (1 - last) + 1 - lax.div(i + PIECES - 1, PIECES)
        return kind, lax.div(i + 1, 2) - 1 + kind

    def products(i):
        kind, g = piece(i)
        for d in range(Y):
            col = pl.ds(pl.multiple_of((y_peer(d) * 4 + g) * B, B), B)
            product = (wide[2 - 2 * kind, :, col].astype(F32) * wide[3 - 2 * kind, :, col].astype(F32)).astype(BF16)
            if d == 0:
                w[g, 2 + kind, pl.ds(pl.multiple_of(y * B, B), B), :] = product
            else:
                s[d - 1, i] = product

    def to_owner(i, d):
        kind, g = piece(i)
        own = pl.ds(pl.multiple_of(y * B, B), B)
        return remote(
            s.at[d - 1, i], w.at[g, 2 + kind, own, :], yi_s.at[i, d - 1], yi_r.at[i, d - 1], at(z, y_peer(d))
        )

    def from_row(i, d):
        kind, g = piece(i)
        theirs = pl.ds(pl.multiple_of(lax.rem(y + Y - d, Y) * B, B), B)
        return remote(
            s.at[d - 1, i], w.at[g, 2 + kind, theirs, :], yi_s.at[i, d - 1], yi_r.at[i, d - 1], at(z, y_peer(d))
        )

    def row_start(i):
        for d in range(1, Y):
            to_owner(i, d).start()

    def row_sent(i):
        for d in range(1, Y):
            to_owner(i, d).wait_send()

    def row_arrive(i):
        for d in range(1, Y):
            from_row(i, d).wait_recv()

    def hop(i, turn):
        kind, g = piece(i)
        to = lax.rem(z + z_count + 1 - 2 * kind, z_count)
        source, target = (2 + kind, 1 + 3 * kind) if turn == 0 else (1 + 3 * kind, 5 * kind)
        return remote(w.at[g, source], w.at[g, target], zs_s.at[i, turn], zs_r.at[i, turn], at(to, y))

    def depth_of(i):
        kind, _ = piece(i)
        return (1 - kind) * z + kind * (z_count - 1 - z)

    def hop_leaves(i, turn):
        return (depth_of(i) >= turn) & (depth_of(i) < z_count - 1)

    def hop_start(i, turn):
        @pl.when(hop_leaves(i, turn))
        def _():
            hop(i, turn).start()

    def hop_arrive(i, turn):
        @pl.when(depth_of(i) >= turn + 1)
        def _():
            hop(i, turn).wait_recv()

    def tap_ring(e, to=near):
        source = ys[e % Y] if isinstance(e, int) else 0
        return remote(placed.at[source], ta.at[e], ta_s.at[e - 1], ta_r.at[e - 1], to)

    def tap_crowd(e, to=near):
        return remote(tb.at[0], tb.at[e], tb_s.at[e - 1], tb_r.at[e - 1], to)

    f_in[...] = jnp.zeros_like(f_in)
    loads[0].wait()
    f_in[0:2, 0 : 4 * Y] = fin[...]
    r16 = lax.broadcasted_iota(jnp.int32, (16, B), 0)
    c16 = lax.broadcasted_iota(jnp.int32, (16, B), 1)
    lane_of = ((c16 == first_lane + r16) & (r16 < 2)).astype(BF16)
    by_group = lax.dot_general(f_in[...], lane_of, (((0,), (0,)), ((), ())), preferred_element_type=F32)
    r32 = lax.broadcasted_iota(jnp.int32, (8 * Y, B), 0)
    c32 = lax.broadcasted_iota(jnp.int32, (8 * Y, B), 1)
    group_of = (c32 == r32 // 8 * 4 + r32 % 4) & (r32 % 8 // 4 == half)
    spots = jnp.dot(group_of.astype(BF16), by_group.astype(BF16), preferred_element_type=F32)
    for q in range(Y):
        placed[q] = spots[q * 8 : q * 8 + 8].astype(BF16)
    ta[0] = placed[y]

    loads[1].wait()
    loads[2].wait()
    products(0)
    pl.semaphore_wait(barrier, (RING - 1) + (crowd - 1))
    for e in range(1, RING):
        tap_ring(e, ring_device(e)).start()

    row_start(0)
    loads[3].wait()
    loads[4].wait()
    for i in range(1, DEPTH):
        products(i)
        row_start(i)

    @pl.loop(DEPTH, PIECES)
    def _(i):
        products(i)

    def arrive(i):
        @pl.when(i + DEPTH < PIECES)
        def _():
            row_sent(i)
            row_start(i + DEPTH)

        row_arrive(i)
        hop_start(i, 0)

    def forward(i):
        hop_arrive(i, 0)
        hop_start(i, 1)

    arrive(0)

    @pl.loop(1, RING)
    def _(e):
        tap_ring(e).wait_recv()

    total = ta[0].astype(F32)
    for e in range(1, RING):
        total = total + ta[e].astype(F32)
    tb[0] = total.astype(BF16)

    for e in range(1, crowd):
        tap_crowd(e, crowd_device(e)).start()

    arrive(1)
    arrive(2)
    forward(0)
    arrive(3)
    forward(1)

    tiles = K // B

    def gather_taps():
        @pl.loop(1, crowd)
        def _(e):
            tap_crowd(e).wait_recv()

        for n in range(x_count):
            total = tb[n * z_count].astype(F32)
            for m in range(1, z_count):
                total = total + tb[n * z_count + m].astype(F32)
            turned = jnp.dot(total.astype(BF16), flip, preferred_element_type=F32)
            for m in range(2):
                j = m * x_count + xs[(x_count - n) % x_count]
                k = tiles - 1 - j
                taps[0, 0:4, pl.ds(pl.multiple_of(j * B, B), B)] = total[m * 4 : m * 4 + 4]
                taps[1, 0:4, pl.ds(pl.multiple_of(k * B, B), B)] = turned[m * 4 : m * 4 + 4]

    def strip_of(g, n):
        line = jnp.concatenate([taps[n, pl.ds(g, 1), :], jnp.zeros((1, B), F32)], axis=1)
        spread = jnp.broadcast_to(line, (B, REACH))
        strips[g, n] = pltpu.roll(spread, n, 1, stride=1, stride_axis=0).astype(BF16)
        return strips[g, n]

    def give_back(i, d):
        kind, g = piece(i)
        to = y_peer(d)
        col = pl.ds(pl.multiple_of((y * 4 + g) * B, B), B)
        return remote(
            o.at[i, pl.ds(pl.multiple_of(to * B, B), B), :], r_ref.at[kind, :, col],
            yo_s.at[i, d - 1], yo_r.at[i, d - 1], at(z, to),
        )

    def get_back(i, d):
        kind, g = piece(i)
        col = pl.ds(pl.multiple_of((lax.rem(y + Y - d, Y) * 4 + g) * B, B), B)
        return remote(
            o.at[i, pl.ds(pl.multiple_of(y_peer(d) * B, B), B), :], r_ref.at[kind, :, col],
            yo_s.at[i, d - 1], yo_r.at[i, d - 1], at(z, y_peer(d)),
        )

    def sum_crowd(e, to=near):
        source = xs[e // z_count] if isinstance(e, int) else 0
        return remote(gp.at[source], sb.at[e - 1], sb_s.at[e - 1], sb_r.at[e - 1], to)

    def sum_ring(e, to=near):
        return remote(sa.at[0], sa.at[e], sa_s.at[e - 1], sa_r.at[e - 1], to)

    def windows(g, first):
        a, b, c = w[g, first], w[g, first + 1], w[g, first + 2]
        return [jnp.concatenate([a[i * B :], b, c[: (i + 1) * B]], axis=0) for i in range(Y)]

    def convolve(i, strip, reach):
        for n in range(Y):
            o[i, n * B : (n + 1) * B, :] = jnp.dot(strip, reach[n], preferred_element_type=F32).astype(BF16)

    def release(first, end):
        @pl.loop(first, end)
        def _(i):
            for d in range(1, Y):
                give_back(i, d).start()

    def correlate(i):
        kind, g = piece(i)
        hop_arrive(i, 1)

        @pl.when(kind == 1)
        def _():
            mixed = w[g, 2]
            across = jnp.concatenate([mixed[n * B : (n + 1) * B] for n in range(Y)], axis=1)
            turned = jnp.dot(flip, across, preferred_element_type=F32).astype(BF16)
            pairs = lax.dot_general(
                turned, jnp.concatenate(windows(g, 3), axis=1), (((1,), (1,)), ((), ())), preferred_element_type=F32
            )
            lined = pltpu.roll(pairs, REACH - (B - 1), 1, stride=1, stride_axis=0)
            lags = jnp.sum(lined, axis=0, keepdims=True)
            for j in range(tiles):
                gp[j % x_count, pl.ds(j // x_count * 4 + g, 1), :] = lags[:, j * B : (j + 1) * B]

            @pl.when(g == 3)
            def _():
                for e in range(1, crowd):
                    sum_crowd(e, crowd_device(e)).start()

    def finish(i):
        kind, g = piece(i)

        @pl.when(kind == 1)
        def _():
            convolve(i, strip_of(g, 0), windows(g, 3))

        @pl.when(kind == 0)
        def _():
            convolve(i, strip_of(g, 1), windows(g, 0))

        col = pl.ds(pl.multiple_of((y * 4 + g) * B, B), B)
        r_ref[kind, :, col] = o[i, pl.ds(pl.multiple_of(y * B, B), B), :]

        @pl.when(i < HELD)
        def _():
            release(i, i + 1)

    @pl.loop(4, PIECES + 4)
    def _(t):
        @pl.when(t < PIECES)
        def _():
            arrive(t)

        @pl.when(t < PIECES + 2)
        def _():
            forward(t - 2)

        correlate(t - 4)

        @pl.when(t == 6)
        def _():
            gather_taps()

            @pl.loop(0, 2)
            def _(i):
                finish(i)

        @pl.when(t >= 6)
        def _():
            finish(t - 4)

    @pl.loop(1, crowd)
    def _(e):
        sum_crowd(e).wait_recv()

    total = gp[x]
    for e in range(1, crowd):
        total = total + sb[e - 1]
    sa[0] = total

    for e in range(1, RING):
        sum_ring(e, ring_device(e)).start()

    release(HELD, PIECES)

    @pl.loop(1, RING)
    def _(e):
        sum_ring(e).wait_recv()

    for d in range(Y):
        total = sa[d]
        for n in range(1, Y):
            total = total + sa[n * Y + d]
        quarters[ys[(Y - d) % Y]] = total
    mine = [jnp.where(half == 0, quarters[q, 0:4], quarters[q, 4:8]) for q in range(Y)]
    hit = lax.broadcasted_iota(jnp.int32, (8, B), 1) == first_lane + lax.broadcasted_iota(jnp.int32, (8, B), 0)
    picked = lax.dot_general(
        hit.astype(F32), jnp.concatenate(mine, axis=0), (((1,), (1,)), ((), ())),
        precision=lax.Precision.HIGHEST, preferred_element_type=F32,
    )
    gout_ref[...] = picked[0:2] / scale

    @pl.loop(0, PIECES)
    def _(i):
        for d in range(1, Y):
            get_back(i, d).wait_recv()
            give_back(i, d).wait_send()
        for turn in range(2):

            @pl.when(hop_leaves(i, turn))
            def _(turn=turn):
                hop(i, turn).wait_send()

    for i in range(PIECES - DEPTH, PIECES):
        row_sent(i)

    @pl.loop(1, RING)
    def _(e):
        tap_ring(e).wait_send()
        sum_ring(e).wait_send()

    @pl.loop(1, crowd)
    def _(e):
        tap_crowd(e).wait_send()
        sum_crowd(e).wait_send()


def shards(pre_gate, post_gate, values, cotangent, filters):
    shard_len, channels = pre_gate.shape[1:]
    groups = filters.shape[1]
    dp_count, seq_count = lax.axis_size("dp"), lax.axis_size("seq")
    z_count, x_count = seq_count // Y, dp_count * Y // RING
    crowd = x_count * z_count
    rows = Y * B
    total_tokens = dp_count * shard_len * seq_count * (channels // groups)

    vmem = pl.BlockSpec(memory_space=pltpu.VMEM)
    hbm = pl.BlockSpec(memory_space=pltpu.HBM)
    dma = pltpu.SemaphoreType.DMA
    operands = (filters, pre_gate[0], post_gate[0], values[0], cotangent[0])
    reached, grad_filters = pl.pallas_call(
        functools.partial(kernel, x_count, z_count, float(total_tokens**0.5)),
        name="hyena",
        out_shape=(
            jax.ShapeDtypeStruct((2, shard_len, channels), BF16),
            jax.ShapeDtypeStruct((2, groups), F32),
        ),
        in_specs=[hbm] * 5,
        out_specs=(vmem, vmem),
        scratch_shapes=[
            pltpu.VMEM((2, groups), BF16),
            pltpu.VMEM((4, shard_len, channels), BF16),
            pltpu.VMEM((16, B), BF16),
            pltpu.VMEM((Y, 8, B), BF16),
            pltpu.VMEM((4, 6, rows, B), BF16),
            pltpu.VMEM((Y - 1, PIECES, B, B), BF16),
            pltpu.VMEM((PIECES, rows, B), BF16),
            pltpu.VMEM((4, 2, B, REACH), BF16),
            pltpu.VMEM((2, 8, K), F32),
            pltpu.VMEM((RING, 8, B), BF16),
            pltpu.VMEM((crowd, 8, B), BF16),
            pltpu.VMEM((x_count, 8, B), F32),
            pltpu.VMEM((crowd - 1, 8, B), F32),
            pltpu.VMEM((RING, 8, B), F32),
            pltpu.VMEM((Y, 8, B), F32),
            dma((5,)),
            dma((PIECES, Y - 1)), dma((PIECES, Y - 1)),
            dma((PIECES, 2)), dma((PIECES, 2)),
            dma((PIECES, Y - 1)), dma((PIECES, Y - 1)),
            dma((RING - 1,)), dma((RING - 1,)),
            dma((crowd - 1,)), dma((crowd - 1,)),
            dma((crowd - 1,)), dma((crowd - 1,)),
            dma((RING - 1,)), dma((RING - 1,)),
        ],
        compiler_params=pltpu.CompilerParams(
            collective_id=0, has_side_effects=True, vmem_limit_bytes=40 << 20
        ),
        cost_estimate=pl.CostEstimate(flops=2 * 10**9, bytes_accessed=4 << 20, transcendentals=0),
    )(*(pltpu.with_memory_space_constraint(operand, pltpu.HBM) for operand in operands))

    convolved, carried = reached[0].astype(F32), reached[1].astype(F32)
    output = (post_gate[0].astype(F32) * convolved).astype(BF16)
    grad_post = (cotangent[0].astype(F32) * convolved).astype(BF16)
    grad_pre = (carried * values[0]).astype(BF16)
    grad_values = (carried * pre_gate[0]).astype(BF16)
    return (output[None], grad_pre[None], grad_post[None], grad_values[None], grad_filters)


def solution(mesh):
    wide = P("dp", "seq", None)
    narrow = P(("dp", "seq"), None)
    return jax.shard_map(
        shards,
        mesh=mesh,
        in_specs=(wide, wide, wide, wide, narrow),
        out_specs=(wide, wide, wide, wide, narrow),
        check_vma=False,
    )
```

```python
import functools

import jax
import jax.numpy as jnp
from jax import lax
from jax.experimental import pallas as pl
from jax.experimental.pallas import tpu as pltpu
from jax.sharding import PartitionSpec as P

K = 1024
B = 128
Y = 4
RING = 16
REACH = K + B
PIECES = 8
DEPTH = 1
HELD = 6
MESH = pl.DeviceIdType.MESH
F32 = jnp.float32
BF16 = jnp.bfloat16


def kernel(
    x_count, z_count, scale,
    f_hbm, pre_hbm, post_hbm, val_hbm, cot_hbm,
    r_ref, gout_ref,
    fin, wide, f_in, placed, w, s, o, strips, taps, ta, tb, gp, sb, sa, quarters,
    in_sem, yi_s, yi_r, zs_s, zs_r, yo_s, yo_r,
    ta_s, ta_r, tb_s, tb_r, sb_s, sb_r, sa_s, sa_r,
):
    dp = lax.axis_index("dp")
    seq = lax.axis_index("seq")
    z, y = seq // Y, seq % Y
    half, x, core = dp // (2 * x_count), dp // 2 % x_count, dp % 2
    rows = Y * B
    crowd = x_count * z_count

    def device(half_to, x_to, core_to, z_to, y_to):
        return {"dp": (half_to * x_count + x_to) * 2 + core_to, "seq": z_to * Y + y_to}

    xs = [lax.rem(x + d, x_count) for d in range(x_count)]
    zs = [lax.rem(z + d, z_count) for d in range(z_count)]
    ys = [lax.rem(y + d, Y) for d in range(Y)]
    halves, cores = (half, 1 - half), (core, 1 - core)

    def y_peer(d):
        return ys[d]

    def at(z_to, y_to):
        return {"dp": dp, "seq": z_to * Y + y_to}

    def ring_device(e):
        return device(halves[e // Y // 2], x, cores[e // Y % 2], z, ys[e % Y])

    def crowd_device(e):
        return device(half, xs[e // z_count], core, zs[e % z_count], y)

    near = at(z, ys[1])

    loads = [pltpu.make_async_copy(f_hbm, fin, in_sem.at[4])]
    for n, ref in enumerate((cot_hbm, post_hbm, pre_hbm, val_hbm)):
        loads.append(pltpu.make_async_copy(ref, wide.at[n], in_sem.at[n]))
    for load in loads:
        load.start()

    barrier = pltpu.get_barrier_semaphore()

    for e in range(1, RING):
        pl.semaphore_signal(barrier, inc=1, device_id=ring_device(e), device_id_type=MESH)
    for e in range(1, crowd):
        pl.semaphore_signal(barrier, inc=1, device_id=crowd_device(e), device_id_type=MESH)

    def remote(src, dst, send, recv, to):
        return pltpu.make_async_remote_copy(
            src_ref=src, dst_ref=dst, send_sem=send, recv_sem=recv, device_id=to, device_id_type=MESH
        )

    empty = jnp.zeros((rows, B), BF16)
    for slot, outside in ((0, z < 2), (1, z < 1), (4, z > z_count - 2), (5, z > z_count - 3)):

        @pl.when(outside)
        def _(slot=slot):
            for g in range(4):
                w[g, slot] = empty

    row_id = lax.broadcasted_iota(jnp.int32, (B, B), 0)
    col_id = lax.broadcasted_iota(jnp.int32, (B, B), 1)
    flip = (row_id + col_id == B - 1).astype(BF16)
    first_lane = core * (B // 2) + 2 * seq

    def piece(i):
        last = lax.div(i, PIECES - 1)
        kind = lax.rem(i, 2) * (1 - last) + 1 - lax.div(i + PIECES - 1, PIECES)
        return kind, lax.div(i + 1, 2) - 1 + kind

    def products(i):
        kind, g = piece(i)
        for d in range(Y):
            col = pl.ds(pl.multiple_of((y_peer(d) * 4 + g) * B, B), B)
            product = (wide[2 - 2 * kind, :, col].astype(F32) * wide[3 - 2 * kind, :, col].astype(F32)).astype(BF16)
            if d == 0:
                w[g, 2 + kind, pl.ds(pl.multiple_of(y * B, B), B), :] = product
            else:
                s[d - 1, i] = product

    def to_owner(i, d):
        kind, g = piece(i)
        own = pl.ds(pl.multiple_of(y * B, B), B)
        return remote(
            s.at[d - 1, i], w.at[g, 2 + kind, own, :], yi_s.at[i, d - 1], yi_r.at[i, d - 1], at(z, y_peer(d))
        )

    def from_row(i, d):
        kind, g = piece(i)
        theirs = pl.ds(pl.multiple_of(lax.rem(y + Y - d, Y) * B, B), B)
        return remote(
            s.at[d - 1, i], w.at[g, 2 + kind, theirs, :], yi_s.at[i, d - 1], yi_r.at[i, d - 1], at(z, y_peer(d))
        )

    def row_start(i):
        for d in range(1, Y):
            to_owner(i, d).start()

    def row_sent(i):
        for d in range(1, Y):
            to_owner(i, d).wait_send()

    def row_arrive(i):
        for d in range(1, Y):
            from_row(i, d).wait_recv()

    def hop(i, turn):
        kind, g = piece(i)
        to = lax.rem(z + z_count + 1 - 2 * kind, z_count)
        source, target = (2 + kind, 1 + 3 * kind) if turn == 0 else (1 + 3 * kind, 5 * kind)
        return remote(w.at[g, source], w.at[g, target], zs_s.at[i, turn], zs_r.at[i, turn], at(to, y))

    def depth_of(i):
        kind, _ = piece(i)
        return (1 - kind) * z + kind * (z_count - 1 - z)

    def hop_leaves(i, turn):
        return (depth_of(i) >= turn) & (depth_of(i) < z_count - 1)

    def hop_start(i, turn):
        @pl.when(hop_leaves(i, turn))
        def _():
            hop(i, turn).start()

    def hop_arrive(i, turn):
        @pl.when(depth_of(i) >= turn + 1)
        def _():
            hop(i, turn).wait_recv()

    def tap_ring(e, to=near):
        source = ys[e % Y] if isinstance(e, int) else 0
        return remote(placed.at[source], ta.at[e], ta_s.at[e - 1], ta_r.at[e - 1], to)

    def tap_crowd(e, to=near):
        return remote(tb.at[0], tb.at[e], tb_s.at[e - 1], tb_r.at[e - 1], to)

    f_in[...] = jnp.zeros_like(f_in)
    loads[0].wait()
    f_in[0:2, 0 : 4 * Y] = fin[...]
    r16 = lax.broadcasted_iota(jnp.int32, (16, B), 0)
    c16 = lax.broadcasted_iota(jnp.int32, (16, B), 1)
    lane_of = ((c16 == first_lane + r16) & (r16 < 2)).astype(BF16)
    by_group = lax.dot_general(f_in[...], lane_of, (((0,), (0,)), ((), ())), preferred_element_type=F32)
    r32 = lax.broadcasted_iota(jnp.int32, (8 * Y, B), 0)
    c32 = lax.broadcasted_iota(jnp.int32, (8 * Y, B), 1)
    group_of = (c32 == r32 // 8 * 4 + r32 % 4) & (r32 % 8 // 4 == half)
    spots = jnp.dot(group_of.astype(BF16), by_group.astype(BF16), preferred_element_type=F32)
    for q in range(Y):
        placed[q] = spots[q * 8 : q * 8 + 8].astype(BF16)
    ta[0] = placed[y]

    loads[1].wait()
    loads[2].wait()
    products(0)
    pl.semaphore_wait(barrier, (RING - 1) + (crowd - 1))
    for e in range(1, RING):
        tap_ring(e, ring_device(e)).start()

    row_start(0)
    loads[3].wait()
    loads[4].wait()
    for i in range(1, DEPTH):
        products(i)
        row_start(i)

    @pl.loop(DEPTH, PIECES)
    def _(i):
        products(i)

    def arrive(i):
        @pl.when(i + DEPTH < PIECES)
        def _():
            row_sent(i)
            row_start(i + DEPTH)

        row_arrive(i)
        hop_start(i, 0)

    def forward(i):
        hop_arrive(i, 0)
        hop_start(i, 1)

    arrive(0)

    @pl.loop(1, RING)
    def _(e):
        tap_ring(e).wait_recv()

    total = ta[0].astype(F32)
    for e in range(1, RING):
        total = total + ta[e].astype(F32)
    tb[0] = total.astype(BF16)

    for e in range(1, crowd):
        tap_crowd(e, crowd_device(e)).start()

    arrive(1)
    arrive(2)
    forward(0)
    arrive(3)
    forward(1)

    tiles = K // B

    def gather_taps():
        @pl.loop(1, crowd)
        def _(e):
            tap_crowd(e).wait_recv()

        for n in range(x_count):
            total = tb[n * z_count].astype(F32)
            for m in range(1, z_count):
                total = total + tb[n * z_count + m].astype(F32)
            turned = jnp.dot(total.astype(BF16), flip, preferred_element_type=F32)
            for m in range(2):
                j = m * x_count + xs[(x_count - n) % x_count]
                k = tiles - 1 - j
                taps[0, 0:4, pl.ds(pl.multiple_of(j * B, B), B)] = total[m * 4 : m * 4 + 4]
                taps[1, 0:4, pl.ds(pl.multiple_of(k * B, B), B)] = turned[m * 4 : m * 4 + 4]

    def strip_of(g, n):
        line = jnp.concatenate([taps[n, pl.ds(g, 1), :], jnp.zeros((1, B), F32)], axis=1)
        spread = jnp.broadcast_to(line, (B, REACH))
        strips[g, n] = pltpu.roll(spread, n, 1, stride=1, stride_axis=0).astype(BF16)
        return strips[g, n]

    def give_back(i, d):
        kind, g = piece(i)
        to = y_peer(d)
        col = pl.ds(pl.multiple_of((y * 4 + g) * B, B), B)
        return remote(
            o.at[i, pl.ds(pl.multiple_of(to * B, B), B), :], r_ref.at[kind, :, col],
            yo_s.at[i, d - 1], yo_r.at[i, d - 1], at(z, to),
        )

    def get_back(i, d):
        kind, g = piece(i)
        col = pl.ds(pl.multiple_of((lax.rem(y + Y - d, Y) * 4 + g) * B, B), B)
        return remote(
            o.at[i, pl.ds(pl.multiple_of(y_peer(d) * B, B), B), :], r_ref.at[kind, :, col],
            yo_s.at[i, d - 1], yo_r.at[i, d - 1], at(z, y_peer(d)),
        )

    def sum_crowd(e, to=near):
        source = xs[e // z_count] if isinstance(e, int) else 0
        return remote(gp.at[source], sb.at[e - 1], sb_s.at[e - 1], sb_r.at[e - 1], to)

    def sum_ring(e, to=near):
        return remote(sa.at[0], sa.at[e], sa_s.at[e - 1], sa_r.at[e - 1], to)

    def windows(g, first):
        a, b, c = w[g, first], w[g, first + 1], w[g, first + 2]
        return [jnp.concatenate([a[i * B :], b, c[: (i + 1) * B]], axis=0) for i in range(Y)]

    def convolve(i, strip, reach):
        for n in range(Y):
            o[i, n * B : (n + 1) * B, :] = jnp.dot(strip, reach[n], preferred_element_type=F32).astype(BF16)

    def release(first, end):
        @pl.loop(first, end)
        def _(i):
            for d in range(1, Y):
                give_back(i, d).start()

    def correlate(i):
        kind, g = piece(i)
        hop_arrive(i, 1)

        @pl.when(kind == 1)
        def _():
            mixed = w[g, 2]
            across = jnp.concatenate([mixed[n * B : (n + 1) * B] for n in range(Y)], axis=1)
            turned = jnp.dot(flip, across, preferred_element_type=F32).astype(BF16)
            pairs = lax.dot_general(
                turned, jnp.concatenate(windows(g, 3), axis=1), (((1,), (1,)), ((), ())), preferred_element_type=F32
            )
            lined = pltpu.roll(pairs, REACH - (B - 1), 1, stride=1, stride_axis=0)
            lags = jnp.sum(lined, axis=0, keepdims=True)
            for j in range(tiles):
                gp[j % x_count, pl.ds(j // x_count * 4 + g, 1), :] = lags[:, j * B : (j + 1) * B]

            @pl.when(g == 3)
            def _():
                for e in range(1, crowd):
                    sum_crowd(e, crowd_device(e)).start()

    def finish(i):
        kind, g = piece(i)

        @pl.when(kind == 1)
        def _():
            convolve(i, strip_of(g, 0), windows(g, 3))

        @pl.when(kind == 0)
        def _():
            convolve(i, strip_of(g, 1), windows(g, 0))

        col = pl.ds(pl.multiple_of((y * 4 + g) * B, B), B)
        r_ref[kind, :, col] = o[i, pl.ds(pl.multiple_of(y * B, B), B), :]

        @pl.when(i < HELD)
        def _():
            release(i, i + 1)

    @pl.loop(4, PIECES + 4)
    def _(t):
        @pl.when(t < PIECES)
        def _():
            arrive(t)

        @pl.when(t < PIECES + 2)
        def _():
            forward(t - 2)

        correlate(t - 4)

        @pl.when(t == 5)
        def _():
            gather_taps()
            finish(0)

        @pl.when(t >= 5)
        def _():
            finish(t - 4)

    @pl.loop(1, crowd)
    def _(e):
        sum_crowd(e).wait_recv()

    total = gp[x]
    for e in range(1, crowd):
        total = total + sb[e - 1]
    sa[0] = total

    for e in range(1, RING):
        sum_ring(e, ring_device(e)).start()

    release(HELD, PIECES)

    @pl.loop(1, RING)
    def _(e):
        sum_ring(e).wait_recv()

    for d in range(Y):
        total = sa[d]
        for n in range(1, Y):
            total = total + sa[n * Y + d]
        quarters[ys[(Y - d) % Y]] = total
    mine = [jnp.where(half == 0, quarters[q, 0:4], quarters[q, 4:8]) for q in range(Y)]
    hit = lax.broadcasted_iota(jnp.int32, (8, B), 1) == first_lane + lax.broadcasted_iota(jnp.int32, (8, B), 0)
    picked = lax.dot_general(
        hit.astype(F32), jnp.concatenate(mine, axis=0), (((1,), (1,)), ((), ())),
        precision=lax.Precision.HIGHEST, preferred_element_type=F32,
    )
    gout_ref[...] = picked[0:2] / scale

    @pl.loop(0, PIECES)
    def _(i):
        for d in range(1, Y):
            get_back(i, d).wait_recv()
            give_back(i, d).wait_send()
        for turn in range(2):

            @pl.when(hop_leaves(i, turn))
            def _(turn=turn):
                hop(i, turn).wait_send()

    for i in range(PIECES - DEPTH, PIECES):
        row_sent(i)

    @pl.loop(1, RING)
    def _(e):
        tap_ring(e).wait_send()
        sum_ring(e).wait_send()

    @pl.loop(1, crowd)
    def _(e):
        tap_crowd(e).wait_send()
        sum_crowd(e).wait_send()


def shards(pre_gate, post_gate, values, cotangent, filters):
    shard_len, channels = pre_gate.shape[1:]
    groups = filters.shape[1]
    dp_count, seq_count = lax.axis_size("dp"), lax.axis_size("seq")
    z_count, x_count = seq_count // Y, dp_count * Y // RING
    crowd = x_count * z_count
    rows = Y * B
    total_tokens = dp_count * shard_len * seq_count * (channels // groups)

    vmem = pl.BlockSpec(memory_space=pltpu.VMEM)
    hbm = pl.BlockSpec(memory_space=pltpu.HBM)
    dma = pltpu.SemaphoreType.DMA
    operands = (filters, pre_gate[0], post_gate[0], values[0], cotangent[0])
    reached, grad_filters = pl.pallas_call(
        functools.partial(kernel, x_count, z_count, float(total_tokens**0.5)),
        name="hyena",
        out_shape=(
            jax.ShapeDtypeStruct((2, shard_len, channels), BF16),
            jax.ShapeDtypeStruct((2, groups), F32),
        ),
        in_specs=[hbm] * 5,
        out_specs=(vmem, vmem),
        scratch_shapes=[
            pltpu.VMEM((2, groups), BF16),
            pltpu.VMEM((4, shard_len, channels), BF16),
            pltpu.VMEM((16, B), BF16),
            pltpu.VMEM((Y, 8, B), BF16),
            pltpu.VMEM((4, 6, rows, B), BF16),
            pltpu.VMEM((Y - 1, PIECES, B, B), BF16),
            pltpu.VMEM((PIECES, rows, B), BF16),
            pltpu.VMEM((4, 2, B, REACH), BF16),
            pltpu.VMEM((2, 8, K), F32),
            pltpu.VMEM((RING, 8, B), BF16),
            pltpu.VMEM((crowd, 8, B), BF16),
            pltpu.VMEM((x_count, 8, B), F32),
            pltpu.VMEM((crowd - 1, 8, B), F32),
            pltpu.VMEM((RING, 8, B), F32),
            pltpu.VMEM((Y, 8, B), F32),
            dma((5,)),
            dma((PIECES, Y - 1)), dma((PIECES, Y - 1)),
            dma((PIECES, 2)), dma((PIECES, 2)),
            dma((PIECES, Y - 1)), dma((PIECES, Y - 1)),
            dma((RING - 1,)), dma((RING - 1,)),
            dma((crowd - 1,)), dma((crowd - 1,)),
            dma((crowd - 1,)), dma((crowd - 1,)),
            dma((RING - 1,)), dma((RING - 1,)),
        ],
        compiler_params=pltpu.CompilerParams(
            collective_id=0, has_side_effects=True, vmem_limit_bytes=40 << 20
        ),
        cost_estimate=pl.CostEstimate(flops=2 * 10**9, bytes_accessed=4 << 20, transcendentals=0),
    )(*(pltpu.with_memory_space_constraint(operand, pltpu.HBM) for operand in operands))

    convolved, carried = reached[0].astype(F32), reached[1].astype(F32)
    output = (post_gate[0].astype(F32) * convolved).astype(BF16)
    grad_post = (cotangent[0].astype(F32) * convolved).astype(BF16)
    grad_pre = (carried * values[0]).astype(BF16)
    grad_values = (carried * pre_gate[0]).astype(BF16)
    return (output[None], grad_pre[None], grad_post[None], grad_values[None], grad_filters)


def solution(mesh):
    wide = P("dp", "seq", None)
    narrow = P(("dp", "seq"), None)
    return jax.shard_map(
        shards,
        mesh=mesh,
        in_specs=(wide, wide, wide, wide, narrow),
        out_specs=(wide, wide, wide, wide, narrow),
        check_vma=False,
    )
```
